32 devices in a mesh: grp: 2 (over y), row: 4 (over x, core), col: 4 (over z).
Axes of the slice: x: 2, y: 2, z: 4, core: 2. Of those that a mesh axis runs over, the one named last changes fastest.
Arguments:
- left_factors: bfloat16 [8, 48, 32, 128], P(('grp', 'row'), 'col'), parts along dimension 0, may hold values from -6 to 6
- right_factors: bfloat16 [8, 48, 32, 128], P(('grp', 'col'), 'row'), parts along dimension 0, may hold values from -6 to 6
- out_weight: bfloat16 [1024, 128], replicated, may hold values from -2 to 2
- out_bias: float32 [128], replicated, may hold values from -4 to 4
- pair_grad: bfloat16 [384, 192, 128], P(('grp', 'row'), 'col'), parts along dimension 0, may hold values from -6 to 6
Outputs:
- pair_update: bfloat16 [384, 192, 128], P(('grp', 'row'), 'col'), parts along dimension 0
- grad_left: float32 [8, 48, 32, 128], P(('grp', 'row'), 'col'), parts along dimension 0
- grad_right: float32 [8, 48, 32, 128], P(('grp', 'col'), 'row'), parts along dimension 0
- grad_weight: float32 [2048, 128], P('grp'), parts along dimension 0
The draws below stay inside these ranges and needn't reach their ends.
There are 2 independent parts, one for each index of `grp`. The reference program is written for one: setup_inputs(seed, part) draws one part's arguments, and reference() takes and returns one part's arrays. A program takes and returns all parts, laid end to end along the dimension named above; an argument that names none is the same for every part. Nothing has to cross between parts.
All inputs are finite; a program needn't handle non-finite values.
Results may differ from the reference program's by a relative error of at most 0.004.
Values may be sent and summed in bfloat16 or wider, within the bound.
A program may use at most 64 MiB of HBM per device.

```python
import jax
import jax.numpy as jnp
from jax import lax

CH = 32
H = 128
S = 128
RES_DEV = 48
K = 1024
L = 192
N_ROW = 4
N_COL = 4


def steps_of(own_key, dims, pieces, low, largest):
    factor_of = 1.0
    for axis_at, shards_of in pieces:
        steps = jax.random.uniform(jax.random.fold_in(jax.random.fold_in(own_key, 6), axis_at), (shards_of,), jnp.float32, low / len(pieces), largest / len(pieces))
        factor_of = factor_of * jnp.repeat(jnp.exp(steps), dims[axis_at] // shards_of).reshape((-1,) + (1,) * (len(dims) - 1 - axis_at))
    return factor_of


def gaussian(stream_key, shape, scale, most, cuts=(), held_as=jnp.bfloat16):
    entries = jax.random.normal(stream_key, shape, jnp.float32) * scale
    if len(cuts) > 0:
        entries = steps_of(stream_key, shape, cuts, -0.22, 0.18) * entries
    return jnp.clip(entries, min=-most, max=most).astype(held_as)


def setup_inputs(seed: int = 0, part: int = 0) -> dict:
    key_of = jax.random.split(jax.random.key(seed), 6)
    own_keys = jax.random.split(jax.random.fold_in(key_of[5], part), 6)
    return {
        "left_factors": gaussian(own_keys[0], (N_ROW, RES_DEV, CH, S), 1.0, 6.0, ((0, 4), (1, 4))),
        "right_factors": gaussian(own_keys[1], (N_COL, RES_DEV, CH, S), 1.0, 6.0, ((0, 4), (1, 4))),
        "out_weight": gaussian(key_of[2], (K, H), (CH * CH // S) ** -0.5, 2.0),
        "out_bias": gaussian(key_of[3], (H,), 1.0, 4.0, (), jnp.float32),
        "pair_grad": gaussian(own_keys[4], (L, L, H), 1.0, 6.0, ((0, 4), (1, 4))),
    }


def reference(left_factors, right_factors, out_weight, out_bias, pair_grad):
    left_all = left_factors.reshape(L, CH, S).astype(jnp.float32)
    right_all = right_factors.reshape(L, CH, S).astype(jnp.float32)
    weight_f = out_weight.astype(jnp.float32)
    row_blocks = left_all.reshape(L // RES_DEV, RES_DEV, CH, S)
    grad_blocks = pair_grad.reshape(L // RES_DEV, RES_DEV, L, H)

    def advance(carried, inputs):
        weight_acc, right_acc = carried
        left_blk, grad_blk = inputs
        outer_mean = (jnp.einsum('ics,jes->ijce', left_blk, right_all) * (1.0 / S)).astype(jnp.bfloat16)
        outer_mean = lax.optimization_barrier(outer_mean)
        outer_f = outer_mean.astype(jnp.float32).reshape(RES_DEV, L, CH * CH)
        pair_blk = (jnp.einsum('ijk,kh->ijh', outer_f, weight_f) + out_bias).astype(jnp.bfloat16)
        grad_f = grad_blk.astype(jnp.float32)
        weight_acc = weight_acc + jnp.einsum('ijk,ijh->kh', outer_f, grad_f)
        outer_grad = jnp.einsum('ijh,kh->ijk', grad_f, weight_f).astype(jnp.bfloat16)
        outer_grad = lax.optimization_barrier(outer_grad)
        outer_grad = outer_grad.astype(jnp.float32).reshape(RES_DEV, L, CH, CH)
        left_part = jnp.einsum('ijce,jes->ics', outer_grad, right_all) * (1.0 / S)
        right_acc = right_acc + jnp.einsum('ijce,ics->jes', outer_grad, left_blk) * (1.0 / S)
        return (weight_acc, right_acc), (pair_blk, left_part)

    start = (jnp.zeros((CH * CH, H), jnp.float32), jnp.zeros((L, CH, S), jnp.float32))
    (weight_acc, right_acc), (pair_blocks, left_parts) = lax.scan(advance, start, (row_blocks, grad_blocks))
    pair_update = pair_blocks.reshape(L, L, H)
    grad_left = left_parts.reshape(N_ROW, RES_DEV, CH, S)
    grad_right = right_acc.reshape(N_COL, RES_DEV, CH, S)
    grad_weight = weight_acc / jnp.float32(L)
    return (pair_update, grad_left, grad_right, grad_weight)
```

```python
import functools

import jax
import jax.numpy as jnp
from jax import lax
from jax.experimental import pallas as pl
from jax.experimental.pallas import tpu as pltpu
from jax.sharding import PartitionSpec as P

BF = jnp.bfloat16
F32 = jnp.float32
MESH = pl.DeviceIdType.MESH
VMEM = pl.BlockSpec(memory_space=pltpu.VMEM)
HBM = pl.BlockSpec(memory_space=pltpu.HBM)


def greet(n_row, n_col, row, col):
    barrier = pltpu.get_barrier_semaphore()
    for d in range(1, n_row):
        pl.semaphore_signal(barrier, inc=1, device_id={"row": lax.rem(row + d, n_row)}, device_id_type=MESH)
    for d in range(1, n_col):
        pl.semaphore_signal(barrier, inc=1, device_id={"col": lax.rem(col + d, n_col)}, device_id_type=MESH)
    pl.semaphore_wait(barrier, n_row + n_col - 2)


def spread(src_of, dst, axis, n, me, send, recv):
    copies = []
    for d in range(1, n):
        to = lax.rem(me + d, n)
        copy = pltpu.make_async_remote_copy(
            src_ref=src_of(to), dst_ref=dst, send_sem=send.at[d - 1], recv_sem=recv.at[d - 1],
            device_id={axis: to}, device_id_type=MESH,
        )
        copy.start()
        copies.append(copy)
    return copies


def send_parts(src_of, slots, axis, n, me, send, recv):
    copies = []
    for d in range(1, n):
        to = lax.rem(me + d, n)
        copy = pltpu.make_async_remote_copy(
            src_ref=src_of(to), dst_ref=slots.at[d - 1], send_sem=send.at[d - 1], recv_sem=recv.at[d - 1],
            device_id={axis: to}, device_id_type=MESH,
        )
        copy.start()
        copies.append(copy)
    return copies


def nn(a, b):
    return lax.dot_general(a, b, (((1,), (0,)), ((), ())), preferred_element_type=F32)


def nt(a, b):
    return lax.dot_general(a, b, (((1,), (1,)), ((), ())), preferred_element_type=F32)


def twice(body):
    def pair_of(p):
        body(p * 2)
        body(p * 2 + 1)

    return pair_of


def whole_kernel(
    n_row, n_col, inv_s, inv_w,
    left_h, right_h, weight_h, bias_h, grad_h,
    pair, sum_l, sum_r, wide, left, right, weight, bias, grad,
    f_rows, f_w, a2, a2t, b2t, wp, wpt, xs, gs, gw_acc, gl_acc, gr_t,
    gl, gr, gw, l_in, r_in, w_in, w_col, w_col_in, w_own, w_half, w_all,
    ls, lr, rs, rr, gls, glr, grs, grr, ws, wr, vs, vr, us, ur, ts, tr, loc,
):
    row, col = lax.axis_index("row"), lax.axis_index("col")
    loads = [
        pltpu.make_async_copy(src, dst, loc.at[at])
        for at, (src, dst) in enumerate((
            (weight_h, weight), (grad_h, grad), (bias_h, bias),
            (right_h, right.at[row]), (left_h, left.at[col]),
        ))
    ]
    for copy in loads:
        copy.start()
    _, piece_l, n_c, n_s = left.shape
    _, piece_r, n_e, _ = right.shape
    n_i, n_j = n_col * piece_l, n_row * piece_r
    n_h = weight.shape[1]
    half = n_i // 2
    pad = 64
    lanes = 2 * pad
    greet(n_row, n_col, row, col)
    c_left = spread(lambda to: left_h, left.at[col], "col", n_col, col, ls, lr)
    c_right = spread(lambda to: right_h, right.at[row], "row", n_row, row, rs, rr)

    loads[0].wait()
    f_w[...] = weight[...].astype(F32).reshape(n_c, n_e, n_h)
    for e in range(n_e):
        wp[e * n_c : (e + 1) * n_c, :] = f_w[:, e, :].astype(BF)
    wpt[...] = wp[...].T
    loads[1].wait()
    loads[2].wait()
    zeros = jnp.zeros((pad - n_j, n_h), BF)

    def grads(ip, count):
        rows = []
        for q in range(count):
            rows += [grad[ip + q], zeros, grad[half + ip + q], zeros]
        return jnp.concatenate(rows, axis=0)

    @pl.loop(0, half // 2)
    def _(p):
        ip = p * 2
        og = nt(wp[...], grads(ip, 2)).astype(BF)
        for q in range(2):
            gs[ip + q] = og[:, q * lanes : (q + 1) * lanes].reshape(n_e, n_c, lanes)

    b2t[...] = jnp.zeros_like(b2t)
    loads[3].wait()
    for copy in c_right:
        copy.wait()
    f_rows[...] = right[...].reshape(n_j, n_e, n_s).astype(F32)
    for e in range(n_e):
        block = f_rows[:, e, :].astype(BF)
        b2t[e, 0:n_j, 0:n_s] = block
        b2t[e, pad : pad + n_j, n_s : 2 * n_s] = block

    gl_acc[...] = jnp.zeros_like(gl_acc)

    @pl.loop(0, n_e // 4)
    def _(p):
        e = p * 4
        g = jnp.concatenate([gs[:, e + q].reshape(half * n_c, lanes) for q in range(4)], axis=1)
        gl_acc[...] += nn(g, b2t[pl.ds(e, 4)].reshape(4 * lanes, 2 * n_s))

    for ii in range(2):
        gl[ii * half : (ii + 1) * half] = gl_acc[:, ii * n_s : (ii + 1) * n_s].reshape(half, n_c, n_s).astype(BF)
    loads[4].wait()
    for copy in c_left:
        copy.wait()
    flat = left[...].reshape(n_i, n_c, n_s)
    for ii in range(2):
        a2[:, ii * n_s : (ii + 1) * n_s] = flat[ii * half : (ii + 1) * half].reshape(half * n_c, n_s)
    c_l = send_parts(lambda to: gl.at[pl.ds(to * piece_l, piece_l)], l_in, "col", n_col, col, gls, glr)

    width = n_e // 2
    rows = width * n_c

    def means(ip, count, first, size):
        return jnp.concatenate(
            [xs[ip + q, first : first + size].reshape(size * n_c, lanes) for q in range(count)], axis=1
        )

    def terms(hf):
        first = hf * width

        def mean(p):
            e = first + p * 2
            out = nt(a2[...], b2t[pl.ds(e, 2)].reshape(2 * lanes, 2 * n_s)).astype(BF)
            for q in range(2):
                xs[:, pl.ds(e + q, 1)] = out[:, q * lanes : (q + 1) * lanes].reshape(half, 1, n_c, lanes)

        pl.loop(0, width // 4)(twice(mean))
        gw_acc[...] = jnp.zeros_like(gw_acc)

        @pl.loop(0, half // 4)
        def _(p):
            gw_acc[...] += nn(means(p * 4, 4, first, width), grads(p * 4, 4))

        gw[hf] = gw_acc[...].reshape(gw.shape[1:]).astype(BF)

    def phase_1(hf):
        return send_parts(lambda to: gw.at[hf, to], w_in.at[hf], "row", n_row, row, ws.at[hf], wr.at[hf])

    def sum_1(hf, copies):
        for copy in copies:
            copy.wait()
        total = gw[hf, row].astype(F32)
        for d in range(n_row - 1):
            total += w_in[hf, d].astype(F32)
        w_col[hf] = total.reshape(w_col.shape[1:]).astype(BF)

    def phase_2(hf):
        return send_parts(lambda to: w_col.at[hf, to], w_col_in.at[hf], "col", n_col, col, vs.at[hf], vr.at[hf])

    def sum_2(hf, copies):
        for copy in copies:
            copy.wait()
        total = w_col[hf, col].astype(F32)
        for d in range(n_col - 1):
            total += w_col_in[hf, d].astype(F32)
        w_own[hf] = (total * inv_w).astype(BF)

    def phase_3(hf):
        mine = pltpu.make_async_copy(w_own.at[hf], w_half.at[hf, col], loc.at[5 + hf])
        mine.start()
        return [mine] + spread(
            lambda to: w_own.at[hf], w_half.at[hf, col], "col", n_col, col, us.at[hf], ur.at[hf]
        )

    def phase_4(hf, copies):
        for copy in copies:
            copy.wait()
        mine = pltpu.make_async_copy(w_half.at[hf], w_all.at[hf, row], loc.at[7 + hf])
        mine.start()
        return [mine] + spread(
            lambda to: w_half.at[hf], w_all.at[hf, row], "row", n_row, row, ts.at[hf], tr.at[hf]
        )

    lane = lax.broadcasted_iota(jnp.int32, (n_s, lanes), 1)

    def rights(p):
        e = p * 2
        g = jnp.concatenate([gs[:, e + q].reshape(half * n_c, lanes) for q in range(2)], axis=1)
        t = nn(a2t[...], g)
        for q in range(2):
            z = jnp.where(
                lane < pad,
                t[0:n_s, q * lanes : (q + 1) * lanes],
                t[n_s : 2 * n_s, q * lanes : (q + 1) * lanes],
            ).T
            gr_t[e + q] = z[0:n_j] + z[pad : pad + n_j]

    def update(p):
        ip = p * 2
        up = nn(wpt[...], means(ip, 2, 0, n_e))
        for q in range(2):
            u = (up[:, q * lanes : (q + 1) * lanes].T * inv_s + bias[...]).astype(BF)
            pair[ip + q] = u[0:n_j]
            pair[half + ip + q] = u[pad : pad + n_j]

    terms(0)
    a2t[...] = a2[...].T
    w_a = phase_1(0)
    terms(1)
    sum_1(0, w_a)
    w_b = phase_1(1)
    w_a = phase_2(0)
    pl.loop(0, width // 4)(twice(rights))
    sum_1(1, w_b)
    sum_2(0, w_a)
    w_b = phase_2(1)
    w_a = phase_3(0)
    pl.loop(width // 4, width // 2)(twice(rights))
    for e in range(n_e):
        f_rows[:, e, :] = gr_t[e]
    gr[...] = f_rows[...].astype(BF)
    sum_2(1, w_b)
    w_a = phase_4(0, w_a)
    w_b = phase_3(1)
    c_r = send_parts(lambda to: gr.at[pl.ds(to * piece_r, piece_r)], r_in, "row", n_row, row, grs, grr)
    early = half // 4 - half // 12
    pl.loop(0, early)(twice(update))
    w_b = phase_4(1, w_b)
    pl.loop(early, half // 4)(twice(update))
    for copy in c_l:
        copy.wait()
    total = gl[pl.ds(col * piece_l, piece_l)].astype(F32)
    for d in range(n_col - 1):
        total += l_in[d].astype(F32)
    sum_l[0] = total * inv_s
    for copy in c_r:
        copy.wait()
    total = gr[pl.ds(row * piece_r, piece_r)].astype(F32)
    for d in range(n_row - 1):
        total += r_in[d].astype(F32)
    sum_r[0] = total * inv_s
    for copy in w_a + w_b:
        copy.wait()
    flat = w_all[...].astype(F32).reshape(n_e, n_c, n_h)
    for e in range(n_e):
        f_w[:, e, :] = flat[e]
    wide[...] = f_w[...].reshape(wide.shape)


def tail_kernel(*refs):
    inner, outer, sems = refs[:4], refs[4:8], refs[8]
    gives = [pltpu.make_async_copy(src, dst, sems.at[at]) for at, (src, dst) in enumerate(zip(inner, outer))]
    for copy in gives:
        copy.start()
    for copy in gives:
        copy.wait()


def dma(n):
    return pltpu.SemaphoreType.DMA((max(n, 1),))


def dma2(n):
    return pltpu.SemaphoreType.DMA((2, n))


def on_device(n_row, n_col, left, right, weight, bias, grad):
    _, piece_l, n_c, n_s = left.shape
    _, piece_r, n_e, _ = right.shape
    n_k, n_h = weight.shape
    n_i, n_j = piece_l * n_col, piece_r * n_row
    half, lanes = n_i // 2, 128
    part = n_k // 2 // n_row
    small = part // n_col
    shapes = (
        jax.ShapeDtypeStruct((n_i, n_j, n_h), BF),
        jax.ShapeDtypeStruct((1, piece_l, n_c, n_s), F32),
        jax.ShapeDtypeStruct((1, piece_r, n_e, n_s), F32),
        jax.ShapeDtypeStruct((n_k, n_h), F32),
    )
    results = pl.pallas_call(
        functools.partial(whole_kernel, n_row, n_col, 1.0 / n_s, 1.0 / (n_s * n_i * n_row)),
        out_shape=tuple(pltpu.VMEM(shape.shape, shape.dtype) for shape in shapes),
        in_specs=[HBM] * 5,
        out_specs=(VMEM,) * 4,
        scratch_shapes=[
            pltpu.VMEM((n_col, piece_l, n_c, n_s), BF),
            pltpu.VMEM((n_row, piece_r, n_e, n_s), BF),
            pltpu.VMEM((n_k, n_h), BF),
            pltpu.VMEM((1, n_h), F32),
            pltpu.VMEM((n_i, n_j, n_h), BF),
            pltpu.VMEM((n_j, n_e, n_s), F32),
            pltpu.VMEM((n_c, n_e, n_h), F32),
            pltpu.VMEM((half * n_c, 2 * n_s), BF),
            pltpu.VMEM((2 * n_s, half * n_c), BF),
            pltpu.VMEM((n_e, lanes, 2 * n_s), BF),
            pltpu.VMEM((n_k, n_h), BF),
            pltpu.VMEM((n_h, n_k), BF),
            pltpu.VMEM((half, n_e, n_c, lanes), BF),
            pltpu.VMEM((half, n_e, n_c, lanes), BF),
            pltpu.VMEM((n_k // 2, n_h), F32),
            pltpu.VMEM((half * n_c, 2 * n_s), F32),
            pltpu.VMEM((n_e, n_j, n_s), F32),
            pltpu.VMEM((n_i, n_c, n_s), BF),
            pltpu.VMEM((n_j, n_e, n_s), BF),
            pltpu.VMEM((2, n_row, part, n_h), BF),
            pltpu.VMEM((n_col - 1, piece_l, n_c, n_s), BF),
            pltpu.VMEM((n_row - 1, piece_r, n_e, n_s), BF),
            pltpu.VMEM((2, n_row - 1, part, n_h), BF),
            pltpu.VMEM((2, n_col, small, n_h), BF),
            pltpu.VMEM((2, n_col - 1, small, n_h), BF),
            pltpu.VMEM((2, small, n_h), BF),
            pltpu.VMEM((2, n_col, small, n_h), BF),
            pltpu.VMEM((2, n_row, n_col, small, n_h), BF),
        ]
        + [dma(n_col)] * 2
        + [dma(n_row)] * 2
        + [dma(n_col)] * 2
        + [dma(n_row)] * 2
        + [dma2(n_row)] * 2
        + [dma2(n_col)] * 4
        + [dma2(n_row)] * 2
        + [dma(9)],
        compiler_params=pltpu.CompilerParams(
            collective_id=0, has_side_effects=True, vmem_limit_bytes=56 * 1024 * 1024
        ),
        name="whole",
    )(left[0], right[0], weight, bias.reshape(1, n_h), grad)
    return pl.pallas_call(
        tail_kernel,
        out_shape=shapes,
        in_specs=[VMEM] * 4,
        out_specs=(HBM,) * 4,
        scratch_shapes=[dma(4)],
        compiler_params=pltpu.CompilerParams(vmem_limit_bytes=1024 * 1024),
        name="tail",
    )(*results)


def solution(mesh):
    return jax.shard_map(
        functools.partial(on_device, mesh.shape["row"], mesh.shape["col"]),
        mesh=mesh,
        in_specs=(
            P(("grp", "row"), "col", None, None),
            P(("grp", "col"), "row", None, None),
            P(),
            P(),
            P(("grp", "row"), "col", None),
        ),
        out_specs=(
            P(("grp", "row"), "col", None),
            P(("grp", "row"), "col", None, None),
            P(("grp", "col"), "row", None, None),
            P("grp", None),
        ),
        check_vma=False,
    )
```

```python
import functools

import jax
import jax.numpy as jnp
from jax import lax
from jax.experimental import pallas as pl
from jax.experimental.pallas import tpu as pltpu
from jax.sharding import PartitionSpec as P

BF = jnp.bfloat16
F32 = jnp.float32
MESH = pl.DeviceIdType.MESH
VMEM = pl.BlockSpec(memory_space=pltpu.VMEM)
HBM = pl.BlockSpec(memory_space=pltpu.HBM)


def greet(n_row, n_col, row, col):
    barrier = pltpu.get_barrier_semaphore()
    for d in range(1, n_row):
        pl.semaphore_signal(barrier, inc=1, device_id={"row": lax.rem(row + d, n_row)}, device_id_type=MESH)
    for d in range(1, n_col):
        pl.semaphore_signal(barrier, inc=1, device_id={"col": lax.rem(col + d, n_col)}, device_id_type=MESH)
    pl.semaphore_wait(barrier, n_row + n_col - 2)


def send(src, dst, axis, to, send_sem, recv_sem):
    pltpu.make_async_remote_copy(
        src_ref=src, dst_ref=dst, send_sem=send_sem, recv_sem=recv_sem,
        device_id={axis: to}, device_id_type=MESH,
    ).start()


def fan(src_of, dst_of, axis, n, me, send_sem, recv_sem):
    for d in range(1, n):
        to = lax.rem(me + d, n)
        send(src_of(to), dst_of(d - 1), axis, to, send_sem, recv_sem)


def take(ref, sem):
    pltpu.make_async_copy(ref, ref, sem).wait()


def nn(a, b):
    return lax.dot_general(a, b, (((1,), (0,)), ((), ())), preferred_element_type=F32)


def nt(a, b):
    return lax.dot_general(a, b, (((1,), (1,)), ((), ())), preferred_element_type=F32)


def twice(body):
    def pair_of(p):
        body(p * 2)
        body(p * 2 + 1)

    return pair_of


def whole_kernel(
    n_row, n_col, inv_s, inv_w,
    left_h, right_h, weight_h, bias_h, grad_h,
    pair, sum_l, sum_r, wide, left, right, weight, bias, grad,
    f_rows, f_w, a2, a2t, b2t, wp, wpt, xs, gs, gw_acc, gl_acc, gr_t,
    gl, gr, gw, l_in, r_in, w_in, w_col, w_col_in, w_own, w_half, w_all,
    sent, l_got, got, w_sent, w_got, loc,
):
    row, col = lax.axis_index("row"), lax.axis_index("col")
    loads = [
        pltpu.make_async_copy(src, dst, loc.at[at])
        for at, (src, dst) in enumerate((
            (weight_h, weight), (grad_h, grad), (bias_h, bias),
            (right_h, right.at[row]), (left_h, left.at[col]),
        ))
    ]
    for copy in loads:
        copy.start()
    _, piece_l, n_c, n_s = left.shape
    _, piece_r, n_e, _ = right.shape
    n_i, n_j = n_col * piece_l, n_row * piece_r
    n_h = weight.shape[1]
    half, many = n_i // 2, piece_l
    pairs, step = n_col // 2, 4 if piece_l % 4 == 0 else piece_l
    pad = 64
    lanes = 2 * pad
    duo = lax.div(col, 2)
    greet(n_row, n_col, row, col)
    send(left_h, left.at[col], "col", col + 1 - 2 * lax.rem(col, 2), sent.at[0], l_got.at[0])
    fan(lambda to: right_h, lambda at: right.at[row], "row", n_row, row, sent.at[1], got.at[0])
    for g in range(1, pairs):
        for b in range(2):
            to = 2 * lax.rem(duo + g, pairs) + b
            send(left_h, left.at[col], "col", to, sent.at[0], l_got.at[pairs - g])

    loads[0].wait()
    f_w[...] = weight[...].astype(F32).reshape(n_c, n_e, n_h)
    for e in range(n_e):
        wp[e * n_c : (e + 1) * n_c, :] = f_w[:, e, :].astype(BF)
    wpt[...] = wp[...].T
    loads[1].wait()
    loads[2].wait()
    zeros = jnp.zeros((pad - n_j, n_h), BF)

    def low(ip):
        return ip + lax.div(ip, many) * many

    def grads(ip, count):
        rows = []
        for q in range(count):
            at = low(ip + q)
            rows += [grad[at], zeros, grad[at + many], zeros]
        return jnp.concatenate(rows, axis=0)

    @pl.loop(0, half // 2)
    def _(p):
        ip = p * 2
        og = nt(wp[...], grads(ip, 2)).astype(BF)
        for q in range(2):
            gs[ip + q] = og[:, q * lanes : (q + 1) * lanes].reshape(n_e, n_c, lanes)

    b2t[...] = jnp.zeros_like(b2t)
    gw_acc[...] = jnp.zeros_like(gw_acc)
    gl_acc[...] = jnp.zeros_like(gl_acc)
    loads[3].wait()
    take(right.at[pl.ds(0, n_row - 1)], got.at[0])
    f_rows[...] = right[...].reshape(n_j, n_e, n_s).astype(F32)
    for e in range(n_e):
        block = f_rows[:, e, :].astype(BF)
        b2t[e, 0:n_j, 0:n_s] = block
        b2t[e, pad : pad + n_j, n_s : 2 * n_s] = block

    width = n_e // 2

    def means(ip, count, first, size):
        return jnp.concatenate(
            [xs[ip + q, first : first + size].reshape(size * n_c, lanes) for q in range(count)], axis=1
        )

    def base_of(g):
        return lax.rem(duo + g, pairs) * many

    def arrive(g):
        at = lax.rem(duo + g, pairs)
        if g == 0:
            loads[4].wait()
            take(left.at[0], l_got.at[0])
        else:
            take(left.at[pl.ds(0, 2)], l_got.at[g])
        for ii in range(2):
            block = left[at * 2 + ii].reshape(many * n_c, n_s)
            a2[pl.ds(at * many * n_c, many * n_c), ii * n_s : (ii + 1) * n_s] = block

    def terms(g, hf):
        base, first = base_of(g), hf * width

        @pl.loop(0, width // 8)
        def _(p):
            rows = a2[pl.ds(base * n_c, many * n_c)]
            for k in range(4):
                e = first + p * 8 + 2 * k
                out = nt(rows, b2t[pl.ds(e, 2)].reshape(2 * lanes, 2 * n_s)).astype(BF)
                for q in range(2):
                    xs[pl.ds(base, many), pl.ds(e + q, 1)] = out[:, q * lanes : (q + 1) * lanes].reshape(
                        many, 1, n_c, lanes
                    )

        @pl.loop(0, many // step)
        def _(p):
            ip = base + p * step
            gw_acc[hf] += nn(means(ip, step, first, width), grads(ip, step))

    def phase_1(hf):
        gw[hf] = gw_acc[hf].reshape(gw.shape[1:]).astype(BF)
        fan(
            lambda to: gw.at[hf, to], lambda at: w_in.at[hf, at], "row", n_row, row,
            w_sent.at[hf], w_got.at[hf],
        )

    def phase_2(hf):
        take(w_in.at[hf], w_got.at[hf])
        total = gw[hf, row].astype(F32)
        for d in range(n_row - 1):
            total += w_in[hf, d].astype(F32)
        w_col[hf] = total.reshape(w_col.shape[1:]).astype(BF)
        fan(
            lambda to: w_col.at[hf, to], lambda at: w_col_in.at[hf, at], "col", n_col, col,
            w_sent.at[2 + hf], w_got.at[2 + hf],
        )

    def phase_3(hf):
        take(w_col_in.at[hf], w_got.at[2 + hf])
        total = w_col[hf, col].astype(F32)
        for d in range(n_col - 1):
            total += w_col_in[hf, d].astype(F32)
        w_own[hf] = (total * inv_w).astype(BF)
        fan(
            lambda to: w_own.at[hf], lambda at: w_half.at[hf, col], "col", n_col, col,
            w_sent.at[4 + hf], w_got.at[4 + hf],
        )
        mine = pltpu.make_async_copy(w_own.at[hf], w_half.at[hf, col], loc.at[5 + hf])
        mine.start()
        return mine

    def phase_4(hf, mine):
        mine.wait()
        take(w_half.at[hf, pl.ds(0, n_col - 1)], w_got.at[4 + hf])
        fan(
            lambda to: w_half.at[hf], lambda at: w_all.at[hf, row], "row", n_row, row,
            w_sent.at[6 + hf], w_got.at[6 + hf],
        )
        mine = pltpu.make_async_copy(w_half.at[hf], w_all.at[hf, row], loc.at[7 + hf])
        mine.start()
        return mine

    def finish(hf, mine):
        mine.wait()
        take(w_all.at[hf, pl.ds(0, n_row - 1)], w_got.at[6 + hf])
        flat = w_all[hf].reshape(width, n_c, n_h)
        for e in range(width):
            wide[:, hf * width + e, :] = flat[e].astype(F32)

    def lefts(p):
        e = p * 4
        g = jnp.concatenate([gs[:, e + q].reshape(half * n_c, lanes) for q in range(4)], axis=1)
        gl_acc[...] += nn(g, b2t[pl.ds(e, 4)].reshape(4 * lanes, 2 * n_s))

    lane = lax.broadcasted_iota(jnp.int32, (n_s, lanes), 1)

    def rights(p):
        e = p * 2
        g = jnp.concatenate([gs[:, e + q].reshape(half * n_c, lanes) for q in range(2)], axis=1)
        t = nn(a2t[...], g)
        for q in range(2):
            z = jnp.where(
                lane < pad,
                t[0:n_s, q * lanes : (q + 1) * lanes],
                t[n_s : 2 * n_s, q * lanes : (q + 1) * lanes],
            ).T
            gr_t[e + q] = z[0:n_j] + z[pad : pad + n_j]

    def give_right(hf):
        for e in range(hf * width, (hf + 1) * width):
            f_rows[:, e, :] = gr_t[e]
        gr[hf] = f_rows[:, hf * width : (hf + 1) * width, :].astype(BF)
        fan(
            lambda to: gr.at[hf, pl.ds(to * piece_r, piece_r)], lambda at: r_in.at[hf, at], "row", n_row, row,
            sent.at[3 + hf], got.at[2 + hf],
        )

    def update(p):
        ip = p * 2
        up = nn(wpt[...], means(ip, 2, 0, n_e))
        for q in range(2):
            u = (up[:, q * lanes : (q + 1) * lanes].T * inv_s + bias[...]).astype(BF)
            at = low(ip + q)
            pair[at] = u[0:n_j]
            pair[at + many] = u[pad : pad + n_j]

    for g in range(pairs):
        arrive(g)
        if g < pairs - 1:
            terms(g, 0)
            terms(g, 1)
    terms(pairs - 1, 0)
    phase_1(0)
    terms(pairs - 1, 1)
    phase_1(1)
    a2t[...] = a2[...].T
    quarter = n_e // 8
    pl.loop(0, quarter)(lefts)
    phase_2(0)
    pl.loop(quarter, 2 * quarter)(lefts)
    phase_2(1)
    for ii in range(2):
        gl[:, ii] = gl_acc[:, ii * n_s : (ii + 1) * n_s].reshape(pairs, many, n_c, n_s).astype(BF)
    fan(lambda to: gl.at[lax.div(to, 2), lax.rem(to, 2)], lambda at: l_in.at[at], "col", n_col, col, sent.at[2], got.at[1])
    pl.loop(0, width // 4)(twice(rights))
    w_a = phase_3(0)
    give_right(0)
    pl.loop(width // 4, width // 2)(twice(rights))
    w_b = phase_3(1)
    give_right(1)
    early = half // 12
    pl.loop(0, early)(twice(update))
    w_a = phase_4(0, w_a)
    pl.loop(early, half // 4)(twice(update))
    w_b = phase_4(1, w_b)
    take(l_in, got.at[1])
    total = gl[duo, lax.rem(col, 2)].astype(F32)
    for d in range(n_col - 1):
        total += l_in[d].astype(F32)
    sum_l[0] = total * inv_s
    finish(0, w_a)
    for hf in range(2):
        take(r_in.at[hf], got.at[2 + hf])
        total = gr[hf, pl.ds(row * piece_r, piece_r)].astype(F32)
        for d in range(n_row - 1):
            total += r_in[hf, d].astype(F32)
        sum_r[0, :, hf * width : (hf + 1) * width, :] = total * inv_s
    finish(1, w_b)
    take(left.at[pl.ds(0, n_col - 1)], sent.at[0])
    take(right.at[pl.ds(0, n_row - 1)], sent.at[1])
    take(l_in, sent.at[2])
    for hf in range(2):
        take(r_in.at[hf], sent.at[3 + hf])
        take(w_in.at[hf], w_sent.at[hf])
        take(w_col_in.at[hf], w_sent.at[2 + hf])
        take(w_half.at[hf, pl.ds(0, n_col - 1)], w_sent.at[4 + hf])
        take(w_all.at[hf, pl.ds(0, n_row - 1)], w_sent.at[6 + hf])


def tail_kernel(*refs):
    inner, outer, sems = refs[:4], refs[4:8], refs[8]
    gives = [pltpu.make_async_copy(src, dst, sems.at[at]) for at, (src, dst) in enumerate(zip(inner, outer))]
    for copy in gives:
        copy.start()
    for copy in gives:
        copy.wait()


def dma(n):
    return pltpu.SemaphoreType.DMA((n,))


def on_device(n_row, n_col, left, right, weight, bias, grad):
    _, piece_l, n_c, n_s = left.shape
    _, piece_r, n_e, _ = right.shape
    n_k, n_h = weight.shape
    n_i, n_j = piece_l * n_col, piece_r * n_row
    half, lanes = n_i // 2, 128
    part = n_k // 2 // n_row
    small = part // n_col
    shapes = (
        jax.ShapeDtypeStruct((n_i, n_j, n_h), BF),
        jax.ShapeDtypeStruct((1, piece_l, n_c, n_s), F32),
        jax.ShapeDtypeStruct((1, piece_r, n_e, n_s), F32),
        jax.ShapeDtypeStruct((n_c, n_e, n_h), F32),
    )
    results = pl.pallas_call(
        functools.partial(whole_kernel, n_row, n_col, 1.0 / n_s, 1.0 / (n_s * n_i * n_row)),
        out_shape=tuple(pltpu.VMEM(shape.shape, shape.dtype) for shape in shapes),
        in_specs=[HBM] * 5,
        out_specs=(VMEM,) * 4,
        scratch_shapes=[
            pltpu.VMEM((n_col, piece_l, n_c, n_s), BF),
            pltpu.VMEM((n_row, piece_r, n_e, n_s), BF),
            pltpu.VMEM((n_k, n_h), BF),
            pltpu.VMEM((1, n_h), F32),
            pltpu.VMEM((n_i, n_j, n_h), BF),
            pltpu.VMEM((n_j, n_e, n_s), F32),
            pltpu.VMEM((n_c, n_e, n_h), F32),
            pltpu.VMEM((half * n_c, 2 * n_s), BF),
            pltpu.VMEM((2 * n_s, half * n_c), BF),
            pltpu.VMEM((n_e, lanes, 2 * n_s), BF),
            pltpu.VMEM((n_k, n_h), BF),
            pltpu.VMEM((n_h, n_k), BF),
            pltpu.VMEM((half, n_e, n_c, lanes), BF),
            pltpu.VMEM((half, n_e, n_c, lanes), BF),
            pltpu.VMEM((2, n_k // 2, n_h), F32),
            pltpu.VMEM((half * n_c, 2 * n_s), F32),
            pltpu.VMEM((n_e, n_j, n_s), F32),
            pltpu.VMEM((n_col // 2, 2, piece_l, n_c, n_s), BF),
            pltpu.VMEM((2, n_j, n_e // 2, n_s), BF),
            pltpu.VMEM((2, n_row, part, n_h), BF),
            pltpu.VMEM((n_col - 1, piece_l, n_c, n_s), BF),
            pltpu.VMEM((2, n_row - 1, piece_r, n_e // 2, n_s), BF),
            pltpu.VMEM((2, n_row - 1, part, n_h), BF),
            pltpu.VMEM((2, n_col, small, n_h), BF),
            pltpu.VMEM((2, n_col - 1, small, n_h), BF),
            pltpu.VMEM((2, small, n_h), BF),
            pltpu.VMEM((2, n_col, small, n_h), BF),
            pltpu.VMEM((2, n_row, n_col, small, n_h), BF),
        ]
        + [dma(5), dma(n_col // 2), dma(4), dma(8), dma(8), dma(9)],
        compiler_params=pltpu.CompilerParams(
            collective_id=0, has_side_effects=True, vmem_limit_bytes=56 * 1024 * 1024
        ),
        name="whole",
    )(left[0], right[0], weight, bias.reshape(1, n_h), grad)
    out_p, out_l, out_r, out_w = pl.pallas_call(
        tail_kernel,
        out_shape=shapes,
        in_specs=[VMEM] * 4,
        out_specs=(HBM,) * 4,
        scratch_shapes=[dma(4)],
        compiler_params=pltpu.CompilerParams(vmem_limit_bytes=1024 * 1024),
        name="tail",
    )(*results)
    return out_p, out_l, out_r, out_w.reshape(n_k, n_h)


def solution(mesh):
    return jax.shard_map(
        functools.partial(on_device, mesh.shape["row"], mesh.shape["col"]),
        mesh=mesh,
        in_specs=(
            P(("grp", "row"), "col", None, None),
            P(("grp", "col"), "row", None, None),
            P(),
            P(),
            P(("grp", "row"), "col", None),
        ),
        out_specs=(
            P(("grp", "row"), "col", None),
            P(("grp", "row"), "col", None, None),
            P(("grp", "col"), "row", None, None),
            P("grp", None),
        ),
        check_vma=False,
    )
```

```python
import functools

import jax
import jax.numpy as jnp
from jax import lax
from jax.experimental import pallas as pl
from jax.experimental.pallas import tpu as pltpu
from jax.sharding import PartitionSpec as P

BF = jnp.bfloat16
F32 = jnp.float32
MESH = pl.DeviceIdType.MESH
VMEM = pl.BlockSpec(memory_space=pltpu.VMEM)
HBM = pl.BlockSpec(memory_space=pltpu.HBM)


def greet(n_row, n_col, row, col):
    barrier = pltpu.get_barrier_semaphore()
    for d in range(1, n_row):
        pl.semaphore_signal(barrier, inc=1, device_id={"row": lax.rem(row + d, n_row)}, device_id_type=MESH)
    for d in range(1, n_col):
        pl.semaphore_signal(barrier, inc=1, device_id={"col": lax.rem(col + d, n_col)}, device_id_type=MESH)
    pl.semaphore_wait(barrier, n_row + n_col - 2)


def send(src, dst, axis, to, send_sem, recv_sem):
    pltpu.make_async_remote_copy(
        src_ref=src, dst_ref=dst, send_sem=send_sem, recv_sem=recv_sem,
        device_id={axis: to}, device_id_type=MESH,
    ).start()


def fan(src_of, dst_of, axis, n, me, send_sem, recv_sem):
    for d in range(1, n):
        to = lax.rem(me + d, n)
        send(src_of(to), dst_of(d - 1), axis, to, send_sem, recv_sem)


def take(ref, sem):
    pltpu.make_async_copy(ref, ref, sem).wait()


def nn(a, b):
    return lax.dot_general(a, b, (((1,), (0,)), ((), ())), preferred_element_type=F32)


def nt(a, b):
    return lax.dot_general(a, b, (((1,), (1,)), ((), ())), preferred_element_type=F32)


def twice(body):
    def pair_of(p):
        body(p * 2)
        body(p * 2 + 1)

    return pair_of


def whole_kernel(
    n_row, n_col, inv_s, inv_w,
    left_h, right_h, weight_h, bias_h, grad_h,
    pair, sum_l, sum_r, wide, left, right, weight, bias, grad,
    f_rows, f_w, a2, a2t, b2t, wp, wpt, xs, gs, gw_acc, gl_acc, gr_t,
    gl, gr, gw, l_in, r_in, w_in, w_col, w_col_in, w_own, w_half, w_all,
    sent, l_got, got, w_sent, w_got, loc,
):
    row, col = lax.axis_index("row"), lax.axis_index("col")
    loads = [
        pltpu.make_async_copy(src, dst, loc.at[at])
        for at, (src, dst) in enumerate((
            (weight_h, weight), (grad_h, grad), (bias_h, bias),
            (right_h, right.at[row]), (left_h, left.at[col]),
        ))
    ]
    for copy in loads:
        copy.start()
    _, piece_l, n_c, n_s = left.shape
    _, piece_r, n_e, _ = right.shape
    n_i, n_j = n_col * piece_l, n_row * piece_r
    n_h = weight.shape[1]
    half, many = n_i // 2, piece_l
    pairs, step = n_col // 2, 4 if piece_l % 4 == 0 else piece_l
    pad = 64
    lanes = 2 * pad
    duo = lax.div(col, 2)
    greet(n_row, n_col, row, col)
    send(left_h, left.at[col], "col", col + 1 - 2 * lax.rem(col, 2), sent.at[0], l_got.at[0])
    fan(lambda to: right_h, lambda at: right.at[row], "row", n_row, row, sent.at[1], got.at[0])
    for g in range(1, pairs):
        for b in range(2):
            to = 2 * lax.rem(duo + g, pairs) + b
            send(left_h, left.at[col], "col", to, sent.at[0], l_got.at[pairs - g])

    loads[0].wait()
    f_w[...] = weight[...].astype(F32).reshape(n_c, n_e, n_h)
    for e in range(n_e):
        wp[e * n_c : (e + 1) * n_c, :] = f_w[:, e, :].astype(BF)
    wpt[...] = wp[...].T
    loads[1].wait()
    loads[2].wait()
    zeros = jnp.zeros((pad - n_j, n_h), BF)

    def low(ip):
        return ip + lax.div(ip, many) * many

    def grads(ip, count):
        rows = []
        for q in range(count):
            at = low(ip + q)
            rows += [grad[at], zeros, grad[at + many], zeros]
        return jnp.concatenate(rows, axis=0)

    @pl.loop(0, half // 2)
    def _(p):
        ip = p * 2
        og = nt(wp[...], grads(ip, 2)).astype(BF)
        for q in range(2):
            gs[ip + q] = og[:, q * lanes : (q + 1) * lanes].reshape(n_e, n_c, lanes)

    b2t[...] = jnp.zeros_like(b2t)
    gw_acc[...] = jnp.zeros_like(gw_acc)
    gl_acc[...] = jnp.zeros_like(gl_acc)
    loads[3].wait()
    take(right.at[pl.ds(0, n_row - 1)], got.at[0])
    f_rows[...] = right[...].reshape(n_j, n_e, n_s).astype(F32)
    for e in range(n_e):
        block = f_rows[:, e, :].astype(BF)
        b2t[e, 0:n_j, 0:n_s] = block
        b2t[e, pad : pad + n_j, n_s : 2 * n_s] = block

    width = n_e // 2

    def means(ip, count, first, size):
        return jnp.concatenate(
            [xs[ip + q, first : first + size].reshape(size * n_c, lanes) for q in range(count)], axis=1
        )

    def base_of(g):
        return lax.rem(duo + g, pairs) * many

    def arrive(g):
        at = lax.rem(duo + g, pairs)
        if g == 0:
            loads[4].wait()
            take(left.at[0], l_got.at[0])
        else:
            take(left.at[pl.ds(0, 2)], l_got.at[g])
        for ii in range(2):
            block = left[at * 2 + ii].reshape(many * n_c, n_s)
            a2[pl.ds(at * many * n_c, many * n_c), ii * n_s : (ii + 1) * n_s] = block

    def terms(g, hf):
        base, first = base_of(g), hf * width

        @pl.loop(0, width // 8)
        def _(p):
            rows = a2[pl.ds(base * n_c, many * n_c)]
            for k in range(4):
                e = first + p * 8 + 2 * k
                out = nt(rows, b2t[pl.ds(e, 2)].reshape(2 * lanes, 2 * n_s)).astype(BF)
                for q in range(2):
                    xs[pl.ds(base, many), pl.ds(e + q, 1)] = out[:, q * lanes : (q + 1) * lanes].reshape(
                        many, 1, n_c, lanes
                    )

        @pl.loop(0, many // step)
        def _(p):
            ip = base + p * step
            gw_acc[hf] += nn(means(ip, step, first, width), grads(ip, step))

    def phase_1(hf):
        gw[hf] = gw_acc[hf].reshape(gw.shape[1:]).astype(BF)
        fan(
            lambda to: gw.at[hf, to], lambda at: w_in.at[hf, at], "row", n_row, row,
            w_sent.at[hf], w_got.at[hf],
        )

    def phase_2(hf):
        take(w_in.at[hf], w_got.at[hf])
        total = gw[hf, row].astype(F32)
        for d in range(n_row - 1):
            total += w_in[hf, d].astype(F32)
        w_col[hf] = total.reshape(w_col.shape[1:]).astype(BF)
        fan(
            lambda to: w_col.at[hf, to], lambda at: w_col_in.at[hf, at], "col", n_col, col,
            w_sent.at[2 + hf], w_got.at[2 + hf],
        )

    def phase_3(hf):
        take(w_col_in.at[hf], w_got.at[2 + hf])
        total = w_col[hf, col].astype(F32)
        for d in range(n_col - 1):
            total += w_col_in[hf, d].astype(F32)
        w_own[hf] = (total * inv_w).astype(BF)
        fan(
            lambda to: w_own.at[hf], lambda at: w_half.at[hf, col], "col", n_col, col,
            w_sent.at[4 + hf], w_got.at[4 + hf],
        )
        mine = pltpu.make_async_copy(w_own.at[hf], w_half.at[hf, col], loc.at[5 + hf])
        mine.start()
        return mine

    def phase_4(hf, mine):
        mine.wait()
        take(w_half.at[hf, pl.ds(0, n_col - 1)], w_got.at[4 + hf])
        fan(
            lambda to: w_half.at[hf], lambda at: w_all.at[hf, row], "row", n_row, row,
            w_sent.at[6 + hf], w_got.at[6 + hf],
        )
        mine = pltpu.make_async_copy(w_half.at[hf], w_all.at[hf, row], loc.at[7 + hf])
        mine.start()
        return mine

    def finish(hf, mine):
        mine.wait()
        take(w_all.at[hf, pl.ds(0, n_row - 1)], w_got.at[6 + hf])
        flat = w_all[hf].reshape(width, n_c, n_h)
        for e in range(width):
            wide[:, hf * width + e, :] = flat[e].astype(F32)

    def lefts(p):
        e = p * 4
        g = jnp.concatenate([gs[:, e + q].reshape(half * n_c, lanes) for q in range(4)], axis=1)
        gl_acc[...] += nn(g, b2t[pl.ds(e, 4)].reshape(4 * lanes, 2 * n_s))

    lane = lax.broadcasted_iota(jnp.int32, (n_s, lanes), 1)

    def rights(p):
        e = p * 2
        g = jnp.concatenate([gs[:, e + q].reshape(half * n_c, lanes) for q in range(2)], axis=1)
        t = nn(a2t[...], g)
        for q in range(2):
            z = jnp.where(
                lane < pad,
                t[0:n_s, q * lanes : (q + 1) * lanes],
                t[n_s : 2 * n_s, q * lanes : (q + 1) * lanes],
            ).T
            gr_t[e + q] = z[0:n_j] + z[pad : pad + n_j]

    def give_right(hf):
        for e in range(hf * width, (hf + 1) * width):
            f_rows[:, e, :] = gr_t[e]
        gr[hf] = f_rows[:, hf * width : (hf + 1) * width, :].astype(BF)
        fan(
            lambda to: gr.at[hf, pl.ds(to * piece_r, piece_r)], lambda at: r_in.at[hf, at], "row", n_row, row,
            sent.at[3 + hf], got.at[2 + hf],
        )

    def update(p):
        ip = p * 2
        up = nn(wpt[...], means(ip, 2, 0, n_e))
        for q in range(2):
            u = (up[:, q * lanes : (q + 1) * lanes].T * inv_s + bias[...]).astype(BF)
            at = low(ip + q)
            pair[at] = u[0:n_j]
            pair[at + many] = u[pad : pad + n_j]

    def trickle(t):
        part = pl.ds(t, 1)
        fan(
            lambda to: gl.at[lax.div(to, 2), lax.rem(to, 2), part], lambda at: l_in.at[at, part],
            "col", n_col, col, sent.at[2], got.at[1],
        )

    def trickling(body, start):
        def trip(p):
            if piece_l < width // 2 + 2 * early:
                pl.when(start + p < piece_l)(lambda: trickle(start + p))
            else:
                trickle(start + p)
            body(p * 2)
            body(p * 2 + 1)

        return trip

    early = half // 12
    for g in range(pairs):
        arrive(g)
        if g < pairs - 1:
            terms(g, 0)
            terms(g, 1)
    terms(pairs - 1, 0)
    phase_1(0)
    terms(pairs - 1, 1)
    phase_1(1)
    a2t[...] = a2[...].T
    quarter = n_e // 8
    pl.loop(0, quarter)(lefts)
    phase_2(0)
    pl.loop(quarter, 2 * quarter)(lefts)
    phase_2(1)
    for ii in range(2):
        gl[:, ii] = gl_acc[:, ii * n_s : (ii + 1) * n_s].reshape(pairs, many, n_c, n_s).astype(BF)
    pl.loop(0, width // 4)(trickling(rights, 0))
    w_a = phase_3(0)
    give_right(0)
    pl.loop(width // 4, width // 2)(trickling(rights, 0))
    w_b = phase_3(1)
    give_right(1)
    pl.loop(0, early)(trickling(update, width // 2))
    w_a = phase_4(0, w_a)
    pl.loop(early, 2 * early)(trickling(update, width // 2))
    pl.loop(2 * early, half // 4)(twice(update))
    for t in range(width // 2 + 2 * early, piece_l):
        trickle(t)
    w_b = phase_4(1, w_b)
    take(l_in, got.at[1])
    total = gl[duo, lax.rem(col, 2)].astype(F32)
    for d in range(n_col - 1):
        total += l_in[d].astype(F32)
    sum_l[0] = total * inv_s
    finish(0, w_a)
    for hf in range(2):
        take(r_in.at[hf], got.at[2 + hf])
        total = gr[hf, pl.ds(row * piece_r, piece_r)].astype(F32)
        for d in range(n_row - 1):
            total += r_in[hf, d].astype(F32)
        sum_r[0, :, hf * width : (hf + 1) * width, :] = total * inv_s
    finish(1, w_b)
    take(left.at[pl.ds(0, n_col - 1)], sent.at[0])
    take(right.at[pl.ds(0, n_row - 1)], sent.at[1])
    take(l_in, sent.at[2])
    for hf in range(2):
        take(r_in.at[hf], sent.at[3 + hf])
        take(w_in.at[hf], w_sent.at[hf])
        take(w_col_in.at[hf], w_sent.at[2 + hf])
        take(w_half.at[hf, pl.ds(0, n_col - 1)], w_sent.at[4 + hf])
        take(w_all.at[hf, pl.ds(0, n_row - 1)], w_sent.at[6 + hf])


def tail_kernel(*refs):
    inner, outer, sems = refs[:4], refs[4:8], refs[8]
    gives = [pltpu.make_async_copy(src, dst, sems.at[at]) for at, (src, dst) in enumerate(zip(inner, outer))]
    for copy in gives:
        copy.start()
    for copy in gives:
        copy.wait()


def dma(n):
    return pltpu.SemaphoreType.DMA((n,))


def on_device(n_row, n_col, left, right, weight, bias, grad):
    _, piece_l, n_c, n_s = left.shape
    _, piece_r, n_e, _ = right.shape
    n_k, n_h = weight.shape
    n_i, n_j = piece_l * n_col, piece_r * n_row
    half, lanes = n_i // 2, 128
    part = n_k // 2 // n_row
    small = part // n_col
    shapes = (
        jax.ShapeDtypeStruct((n_i, n_j, n_h), BF),
        jax.ShapeDtypeStruct((1, piece_l, n_c, n_s), F32),
        jax.ShapeDtypeStruct((1, piece_r, n_e, n_s), F32),
        jax.ShapeDtypeStruct((n_c, n_e, n_h), F32),
    )
    results = pl.pallas_call(
        functools.partial(whole_kernel, n_row, n_col, 1.0 / n_s, 1.0 / (n_s * n_i * n_row)),
        out_shape=tuple(pltpu.VMEM(shape.shape, shape.dtype) for shape in shapes),
        in_specs=[HBM] * 5,
        out_specs=(VMEM,) * 4,
        scratch_shapes=[
            pltpu.VMEM((n_col, piece_l, n_c, n_s), BF),
            pltpu.VMEM((n_row, piece_r, n_e, n_s), BF),
            pltpu.VMEM((n_k, n_h), BF),
            pltpu.VMEM((1, n_h), F32),
            pltpu.VMEM((n_i, n_j, n_h), BF),
            pltpu.VMEM((n_j, n_e, n_s), F32),
            pltpu.VMEM((n_c, n_e, n_h), F32),
            pltpu.VMEM((half * n_c, 2 * n_s), BF),
            pltpu.VMEM((2 * n_s, half * n_c), BF),
            pltpu.VMEM((n_e, lanes, 2 * n_s), BF),
            pltpu.VMEM((n_k, n_h), BF),
            pltpu.VMEM((n_h, n_k), BF),
            pltpu.VMEM((half, n_e, n_c, lanes), BF),
            pltpu.VMEM((half, n_e, n_c, lanes), BF),
            pltpu.VMEM((2, n_k // 2, n_h), F32),
            pltpu.VMEM((half * n_c, 2 * n_s), F32),
            pltpu.VMEM((n_e, n_j, n_s), F32),
            pltpu.VMEM((n_col // 2, 2, piece_l, n_c, n_s), BF),
            pltpu.VMEM((2, n_j, n_e // 2, n_s), BF),
            pltpu.VMEM((2, n_row, part, n_h), BF),
            pltpu.VMEM((n_col - 1, piece_l, n_c, n_s), BF),
            pltpu.VMEM((2, n_row - 1, piece_r, n_e // 2, n_s), BF),
            pltpu.VMEM((2, n_row - 1, part, n_h), BF),
            pltpu.VMEM((2, n_col, small, n_h), BF),
            pltpu.VMEM((2, n_col - 1, small, n_h), BF),
            pltpu.VMEM((2, small, n_h), BF),
            pltpu.VMEM((2, n_col, small, n_h), BF),
            pltpu.VMEM((2, n_row, n_col, small, n_h), BF),
        ]
        + [dma(5), dma(n_col // 2), dma(4), dma(8), dma(8), dma(9)],
        compiler_params=pltpu.CompilerParams(
            collective_id=0, has_side_effects=True, vmem_limit_bytes=56 * 1024 * 1024
        ),
        name="whole",
    )(left[0], right[0], weight, bias.reshape(1, n_h), grad)
    out_p, out_l, out_r, out_w = pl.pallas_call(
        tail_kernel,
        out_shape=shapes,
        in_specs=[VMEM] * 4,
        out_specs=(HBM,) * 4,
        scratch_shapes=[dma(4)],
        compiler_params=pltpu.CompilerParams(vmem_limit_bytes=1024 * 1024),
        name="tail",
    )(*results)
    return out_p, out_l, out_r, out_w.reshape(n_k, n_h)


def solution(mesh):
    return jax.shard_map(
        functools.partial(on_device, mesh.shape["row"], mesh.shape["col"]),
        mesh=mesh,
        in_specs=(
            P(("grp", "row"), "col", None, None),
            P(("grp", "col"), "row", None, None),
            P(),
            P(),
            P(("grp", "row"), "col", None),
        ),
        out_specs=(
            P(("grp", "row"), "col", None),
            P(("grp", "row"), "col", None, None),
            P(("grp", "col"), "row", None, None),
            P("grp", None),
        ),
        check_vma=False,
    )
```
